256 devices in a mesh: group: 32 (over z, x), row: 8 (over y, core).
Axes of the slice: x: 4, y: 4, z: 8, core: 2. Of those that a mesh axis runs over, the one named last changes fastest.
Arguments:
- video_frames: bfloat16 [128, 32, 192, 128], P('group', 'row'), may hold values from -6 to 6
- pred_owner: int32 [32], P('group'), may hold values from -1 to 30, as said below
- frame_counts: int32 [32], P('group'), may hold values from 2 to 4, as said below
- norm1_gain: float32 [128], replicated, may hold values from 0.1 to 1.9
- conv1_weight: bfloat16 [3, 3, 3, 128, 128], replicated, may hold values from -0.109375 to 0.109375
- conv1_bias: float32 [128], replicated, may hold values from -3 to 3
- norm2_gain: float32 [128], replicated, may hold values from 0.1 to 1.9
- conv2_weight: bfloat16 [3, 3, 3, 128, 256], replicated, may hold values from -0.109375 to 0.109375
- conv2_bias: float32 [256], replicated, may hold values from -3 to 3
Outputs:
- encoded: bfloat16 [64, 16, 96, 256], P('group', 'row')
The draws below stay inside these ranges and needn't reach their ends.
Inputs may be any that keep to these rules, and one draw needn't show every extreme that they name: `pred_owner`: -1 marks a video's first group; otherwise it is the nearest earlier group of the same video, 1 to 4 groups earlier. No group is the predecessor of two groups. Group 0 has none. `frame_counts`: every count is even; a group that precedes another group holds 4 frames, only a video's last group may hold fewer.
All inputs are finite; a program needn't handle non-finite values.
Results may differ from the reference program's by a relative error of at most 0.0046.
Values may be sent and summed in bfloat16 or wider, within the bound.
A program may use at most 64 MiB of HBM per device.

```python
import jax
import jax.numpy as jnp
from jax import lax

C = 128
C2 = 256
FR = 4
W = 192
SPAN = 4
FRAMES = 128
H = 32
N_GROUP = 32


def chain_owners(key):
    positions = jnp.arange(N_GROUP, dtype=jnp.int32)
    stream_key, start_key = jax.random.split(jax.random.fold_in(key, 11))
    streams = jax.random.randint(stream_key, (N_GROUP,), 0, SPAN, dtype=jnp.int32)
    streams = jnp.where(positions < SPAN, positions, streams)
    streams = jnp.where(positions == SPAN, 0, streams)
    streams = jnp.where(positions == N_GROUP - 1, streams[N_GROUP - 2], streams)
    owners = jnp.full((N_GROUP,), -1, jnp.int32)
    for offset in reversed(range(1, SPAN + 1)):
        earlier = jnp.roll(streams, offset)
        match = (earlier == streams) & (positions >= offset)
        owners = jnp.where(match, positions - offset, owners)
    starts = jax.random.randint(start_key, (N_GROUP,), 0, 4, dtype=jnp.int32) == 0
    forced = (positions == SPAN) | (positions == N_GROUP - 1)
    return jnp.where(starts & ~forced, -1, owners).astype(jnp.int32)


def draw_pred_owner(key, part):
    return chain_owners(key)


def draw_frame_counts(key, part):
    positions = jnp.arange(N_GROUP, dtype=jnp.int32)
    owners = chain_owners(key)
    has_next = jnp.any(owners[None, :] == positions[:, None], axis=1)
    halves = jax.random.randint(jax.random.fold_in(key, 23), (N_GROUP,), 1, FR // 2 + 1, dtype=jnp.int32)
    halves = jnp.where(positions == N_GROUP - 1, 1, halves)
    return jnp.where(has_next, FR, 2 * halves).astype(jnp.int32)


def shard_levels(rng, dims, pieces, smallest, largest):
    gain, own = 1.0, jax.random.fold_in(rng, 6)
    for position, shards_of in pieces:
        steps = jnp.exp(jax.random.uniform(jax.random.fold_in(own, position), (shards_of,), jnp.float32, smallest / len(pieces), largest / len(pieces)))
        gain = gain * jnp.repeat(steps, dims[position] // shards_of).reshape([-1 if axis == position else 1 for axis in range(len(dims))])
    return gain


def normal_values(key, dims, scale, limit, shards=(), kind=jnp.bfloat16):
    drawn = jax.random.normal(key, dims, jnp.float32) * scale
    if len(shards) > 0:
        drawn = shard_levels(key, dims, shards, -0.22, 0.18) * drawn
    return jnp.clip(drawn, min=-limit, max=limit).astype(kind)


def setup_inputs(seed: int = 0) -> dict:
    splits = jax.random.split(jax.random.key(seed), 10)
    return {
        "video_frames": normal_values(splits[0], (FRAMES, H, W, C), 1.0, 6.0, ((0, 32), (1, 8))),
        "pred_owner": draw_pred_owner(jax.random.fold_in(splits[9], 71), 0),
        "frame_counts": draw_frame_counts(jax.random.fold_in(splits[9], 71), 0),
        "norm1_gain": jnp.clip(1.0 + 0.18 * jax.random.normal(splits[3], (C,), jnp.float32), 0.1, 1.9),
        "conv1_weight": normal_values(splits[4], (3, 3, 3, C, C), (27 * C) ** -0.5, 0.109375),
        "conv1_bias": normal_values(splits[5], (C,), 0.5, 3.0, (), jnp.float32),
        "norm2_gain": jnp.clip(1.0 + 0.18 * jax.random.normal(splits[6], (C,), jnp.float32), 0.1, 1.9),
        "conv2_weight": normal_values(splits[7], (3, 3, 3, C, C2), (27 * C) ** -0.5, 0.109375),
        "conv2_bias": normal_values(splits[8], (C2,), 0.5, 3.0, (), jnp.float32),
    }


def prepare(values, norm_gain):
    values = values.astype(jnp.float32)
    inverse = lax.rsqrt(lax.optimization_barrier(jnp.mean(values * values, axis=-1, keepdims=True)) + 1e-06)
    return jax.nn.silu(values * inverse * norm_gain).astype(jnp.bfloat16)

def conv_steady(padded, weight, out_frames, out_rows):
    channels = padded.shape[-1]
    columns = padded.shape[2] - 2
    outputs = weight.shape[-1]
    summed = jnp.zeros((out_frames * out_rows * columns, outputs), jnp.float32)
    for step_t in range(3):
        for step_h in range(3):
            window = jnp.concatenate([padded[step_t:step_t + out_frames, step_h:step_h + out_rows, step_w:step_w + columns] for step_w in range(3)], axis=-1)
            flattened = window.reshape(out_frames * out_rows * columns, 3 * channels)
            summed = summed + jnp.dot(flattened, weight[step_t, step_h].reshape(3 * channels, outputs), preferred_element_type=jnp.float32)
    return summed.reshape(out_frames, out_rows, columns, outputs)

def conv_stride(padded, weight, out_frames, out_rows):
    channels = padded.shape[-1]
    out_cols = (padded.shape[2] - 2) // 2
    outputs = weight.shape[-1]
    summed = jnp.zeros((out_frames * out_rows * out_cols, outputs), jnp.float32)
    for step_t in range(3):
        for step_h in range(3):
            window = jnp.concatenate([padded[step_t:step_t + 2 * out_frames:2, step_h:step_h + 2 * out_rows:2, step_w:step_w + 2 * out_cols:2] for step_w in range(3)], axis=-1)
            flattened = window.reshape(out_frames * out_rows * out_cols, 3 * channels)
            summed = summed + jnp.dot(flattened, weight[step_t, step_h].reshape(3 * channels, outputs), preferred_element_type=jnp.float32)
    return summed.reshape(out_frames, out_rows, out_cols, outputs)

def last_frames(clip, valid_count, amount):
    return lax.dynamic_slice_in_dim(clip, (valid_count - amount).astype(jnp.int32), amount, 0)

def reference(video_frames, pred_owner, frame_counts, norm1_gain, conv1_weight, conv1_bias, norm2_gain, conv2_weight, conv2_bias):
    groups = pred_owner.shape[0]
    rows = video_frames.shape[1]
    columns = video_frames.shape[2]
    channels = video_frames.shape[3]
    clips = video_frames.reshape(groups, FR, rows, columns, channels)
    source = jnp.maximum(pred_owner, 0).astype(jnp.int32)
    has_prior = (pred_owner >= 0)[:, None, None, None, None]
    hidden = prepare(clips, norm1_gain)
    tails_one = jax.vmap(lambda clip, valid_count: last_frames(clip, valid_count, 2))(hidden, frame_counts)
    before_one = jnp.where(has_prior, tails_one[source], jnp.zeros_like(tails_one))

    def layer_one(item):
        prior, clip, inputs = item
        extended = jnp.concatenate([prior, clip], 0)
        padded = jnp.pad(extended, ((0, 0), (1, 1), (1, 1), (0, 0)))
        mixed = conv_steady(padded, conv1_weight, FR, rows)
        return prepare(inputs.astype(jnp.float32) + mixed + conv1_bias, norm2_gain)
    second = lax.map(layer_one, (before_one, hidden, clips))
    tails_two = jax.vmap(lambda clip, valid_count: last_frames(clip, valid_count, 1))(second, frame_counts)
    before_two = jnp.where(has_prior, tails_two[source], jnp.zeros_like(tails_two))

    def layer_two(item):
        prior, clip, valid_count = item
        extended = jnp.concatenate([prior, clip], 0)
        padded = jnp.pad(extended, ((0, 0), (1, 0), (1, 1), (0, 0)))
        mixed = conv_stride(padded, conv2_weight, FR // 2, rows // 2) + conv2_bias
        keep = jnp.arange(FR // 2) < valid_count // 2
        return jnp.where(keep[:, None, None, None], mixed, 0.0).astype(jnp.bfloat16)
    encoded = lax.map(layer_two, (before_two, second, frame_counts))
    return encoded.reshape(groups * (FR // 2), rows // 2, columns // 2, conv2_weight.shape[-1])
```

```python
import functools

import jax
import jax.numpy as jnp
from jax import lax
from jax.experimental import pallas as pl
from jax.experimental.pallas import tpu as pltpu
from jax.sharding import PartitionSpec as P

MESH = pl.DeviceIdType.MESH
NX = 4
ROWS = 4
F32 = jnp.float32
BF16 = jnp.bfloat16


def prepare(v, gain):
    inverse = lax.rsqrt(jnp.mean(v * v, axis=-1, keepdims=True) + 1e-06)
    half = v * inverse * (0.5 * gain)
    return half * (1.0 + jnp.tanh(half))


def kernel(
    n_group, n_row, x_hbm, po_ref, fc_ref, g1_ref, w1_hbm, b1_ref, g2_ref, w2_hbm, b2_ref, out_ref,
    xv, w1v, w2v, hid, hin, zb, tmp, sec, sin, enc,
    tb, rl, rr, r2, zs, zr, eb, el, er, e2, es, ez, info_s, info_r,
    lsem, hsend, hrecv, ssend, srecv, isend, irecv, xsend, xrecv, ysend, yrecv, zsend, zrecv,
):
    width = xv.shape[2]
    half_w = width // 2
    n_z = n_group // NX
    me = lax.axis_index("group")
    row = lax.axis_index("row")
    z = me // NX
    x = me % NX
    right = (z * NX + (x + 1) % NX, row)
    left = (z * NX + (x + 3) % NX, row)
    above_z = (((z + 1) % n_z) * NX + x, row)
    below_z = (((z + n_z - 1) % n_z) * NX + x, row)
    up = (me, jnp.maximum(row - 1, 0))
    down = (me, jnp.minimum(row + 1, n_row - 1))
    has_up = row > 0
    has_down = row < n_row - 1

    barrier = pltpu.get_barrier_semaphore()
    for dev in (right, left, above_z, below_z):
        pl.semaphore_signal(barrier, inc=1, device_id=dev, device_id_type=MESH)

    @pl.when(has_up)
    def _():
        pl.semaphore_signal(barrier, inc=1, device_id=up, device_id_type=MESH)

    @pl.when(has_down)
    def _():
        pl.semaphore_signal(barrier, inc=1, device_id=down, device_id_type=MESH)

    loads = [
        pltpu.make_async_copy(x_hbm.at[2:4], xv.at[2:4], lsem.at[0]),
        pltpu.make_async_copy(w1_hbm.at[2], w1v.at[:, 0:128], lsem.at[1]),
        pltpu.make_async_copy(w1_hbm.at[1], w1v.at[:, 128:256], lsem.at[2]),
        pltpu.make_async_copy(w1_hbm.at[0], w1v.at[:, 256:384], lsem.at[3]),
        pltpu.make_async_copy(x_hbm.at[0:2], xv.at[0:2], lsem.at[4]),
        pltpu.make_async_copy(w2_hbm, w2v, lsem.at[5]),
    ]
    for load in loads:
        load.start()

    pred = po_ref[0]
    info_s[...] = jnp.full((8, 128), pred, jnp.int32)

    columns = lax.broadcasted_iota(jnp.int32, (width, 128), 0)
    half_columns = lax.broadcasted_iota(jnp.int32, (half_w, 128), 0)

    def store_hidden(f, r, h):
        before = jnp.where(columns == 0, 0.0, pltpu.roll(h, 1, 0))
        after = jnp.where(columns == width - 1, 0.0, pltpu.roll(h, width - 1, 0))
        hid[f, r, :, 0:128] = before.astype(BF16)
        hid[f, r, :, 128:256] = h.astype(BF16)
        hid[f, r, :, 256:384] = after.astype(BF16)

    gain1 = g1_ref[...]
    gain2 = g2_ref[...]

    def hidden_frames(base):
        def step(i, carry):
            f = base + i // ROWS
            r = i % ROWS
            store_hidden(f, r + 1, prepare(xv[f, r].astype(F32), gain1))
            return carry

        lax.fori_loop(0, 2 * ROWS, step, 0, unroll=2)

    def halo_copies(base, batch):
        to_up = pltpu.make_async_remote_copy(
            src_ref=hid.at[base : base + 2, 1, :, 128:256], dst_ref=hin.at[1, base : base + 2],
            send_sem=hsend.at[batch, 0], recv_sem=hrecv.at[batch, 1], device_id=up, device_id_type=MESH,
        )
        to_down = pltpu.make_async_remote_copy(
            src_ref=hid.at[base : base + 2, ROWS, :, 128:256], dst_ref=hin.at[0, base : base + 2],
            send_sem=hsend.at[batch, 1], recv_sem=hrecv.at[batch, 0], device_id=down, device_id_type=MESH,
        )
        return to_up, to_down

    def send_halo(base, batch):
        to_up, to_down = halo_copies(base, batch)

        @pl.when(has_up)
        def _():
            to_up.start()

        @pl.when(has_down)
        def _():
            to_down.start()

    def receive_halo(base, batch):
        to_up, to_down = halo_copies(base, batch)

        @pl.when(has_up)
        def _():
            to_down.wait_recv()
            for f in (base, base + 1):
                store_hidden(f, 0, hin[0, f].astype(F32))

        @pl.when(has_down)
        def _():
            to_up.wait_recv()
            for f in (base, base + 1):
                store_hidden(f, ROWS + 1, hin[1, f].astype(F32))

        @pl.when(row == 0)
        def _():
            for f in (base, base + 1):
                hid[f, 0] = jnp.zeros((width, 384), BF16)

        @pl.when(row == n_row - 1)
        def _():
            for f in (base, base + 1):
                hid[f, ROWS + 1] = jnp.zeros((width, 384), BF16)

    def products(base, r):
        lhs = jnp.concatenate(
            [
                jnp.concatenate([hid[f, r + b] for b in range(3)], axis=1)
                for f in (base, base + 1)
            ],
            axis=0,
        )
        made = jnp.dot(lhs, w1v[...], preferred_element_type=F32)
        zb[base, r] = made[:width]
        zb[base + 1, r] = made[width:]

    def direct_copies(src, from_left, from_right, c):
        return (
            pltpu.make_async_remote_copy(
                src_ref=src, dst_ref=from_left, send_sem=xsend.at[c, 0], recv_sem=xrecv.at[c, 0],
                device_id=right, device_id_type=MESH,
            ),
            pltpu.make_async_remote_copy(
                src_ref=src, dst_ref=from_right, send_sem=xsend.at[c, 1], recv_sem=xrecv.at[c, 1],
                device_id=left, device_id_type=MESH,
            ),
        )

    def relay_copies(from_left, from_right, far, c):
        return (
            pltpu.make_async_remote_copy(
                src_ref=from_left.at[0], dst_ref=far.at[0], send_sem=ysend.at[c, 0], recv_sem=yrecv.at[c, 0],
                device_id=right, device_id_type=MESH,
            ),
            pltpu.make_async_remote_copy(
                src_ref=from_right.at[1], dst_ref=far.at[1], send_sem=ysend.at[c, 1], recv_sem=yrecv.at[c, 1],
                device_id=left, device_id_type=MESH,
            ),
        )

    def z_copy(src, dst, c):
        return pltpu.make_async_remote_copy(
            src_ref=src, dst_ref=dst, send_sem=zsend.at[c], recv_sem=zrecv.at[c],
            device_id=above_z, device_id_type=MESH,
        )

    info = pltpu.make_async_remote_copy(
        src_ref=info_s, dst_ref=info_r, send_sem=isend.at[0], recv_sem=irecv.at[0],
        device_id=below_z, device_id_type=MESH,
    )
    direct = [direct_copies(tb.at[c], rl.at[c], rr.at[c], c) for c in range(ROWS)]
    direct.append(direct_copies(eb, el, er, ROWS))
    relays = [relay_copies(rl.at[c], rr.at[c], r2.at[c], c) for c in range(ROWS)]
    relays.append(relay_copies(el, er, e2, ROWS))
    ups = [z_copy(zs.at[c], zr.at[c], c) for c in range(ROWS)]
    ups.append(z_copy(es, ez, ROWS))

    def send_contributions(r):
        tb[r, 0] = (zb[2, r, :, 256:384] + zb[3, r, :, 128:256]).astype(BF16)
        tb[r, 1] = zb[3, r, :, 256:384].astype(BF16)
        for copy in direct[r]:
            copy.start()

    def relay(c):
        for copy, on in zip(direct[c], relays[c]):
            copy.wait_recv()
            on.start()

    def pick(c, which, own, from_left, far, from_right):
        kept = jnp.where(which == 0, own[...], from_left[...])
        kept = jnp.where(which == 2, far[...], kept)
        return jnp.where(which == 3, from_right[...], kept)

    def send_up(c, which):
        for copy in relays[c]:
            copy.wait_recv()
        if c < ROWS:
            zs[c] = pick(c, which, tb.at[c], rl.at[c], r2.at[c], rr.at[c])
        else:
            es[...] = pick(c, which, eb, el, e2, er)
        ups[c].start()

    distance = me - pred
    choice = jnp.where(pred < 0, 5, jnp.where(distance <= x, distance, 0))

    def received(c):
        ups[c].wait_recv()
        if c < ROWS:
            got = pick(c, choice, zr.at[c], rl.at[c], r2.at[c], rr.at[c])
        else:
            got = pick(c, choice, ez, el, e2, er)
        got = got.astype(F32)
        return jnp.where(choice == 5, 0.0, got)

    bias1 = b1_ref[...]

    def store_second(t, r, mixed):
        v = xv[t, r].astype(F32) + mixed + bias1
        slot = tmp.at[t % 2]
        slot[...] = prepare(v, gain2)
        even = slot[pl.ds(0, half_w, stride=2), :]
        odd = slot[pl.ds(1, half_w, stride=2), :]
        sec[t, r + 1, :, 0:128] = jnp.where(half_columns == 0, 0.0, pltpu.roll(odd, 1, 0)).astype(BF16)
        sec[t, r + 1, :, 128:256] = even.astype(BF16)
        sec[t, r + 1, :, 256:384] = odd.astype(BF16)

    def second_copy(base, batch):
        return pltpu.make_async_remote_copy(
            src_ref=sec.at[base : base + 2, ROWS, :, 128:384], dst_ref=sin.at[base : base + 2],
            send_sem=ssend.at[batch], recv_sem=srecv.at[batch], device_id=down, device_id_type=MESH,
        )

    def send_second(base, batch):
        @pl.when(has_down)
        def _():
            second_copy(base, batch).start()

    def receive_second(base, batch):
        @pl.when(has_up)
        def _():
            second_copy(base, batch).wait_recv()
            for t in (base, base + 1):
                odd = sin[t, :, 128:256].astype(F32)
                sec[t, 0, :, 0:128] = jnp.where(half_columns == 0, 0.0, pltpu.roll(odd, 1, 0)).astype(BF16)
                sec[t, 0, :, 128:384] = sin[t]

        @pl.when(row == 0)
        def _():
            for t in (base, base + 1):
                sec[t, 0] = jnp.zeros((half_w, 384), BF16)

    def downsample(t, a):
        lhs = jnp.concatenate(
            [
                jnp.concatenate([sec[t, 2 * i + b] for b in range(3)], axis=1)
                for i in range(2)
            ],
            axis=0,
        )
        return jnp.dot(lhs, w2v[a], preferred_element_type=F32)

    loads[0].wait()
    hidden_frames(2)
    pl.semaphore_wait(barrier, 4 + has_up.astype(jnp.int32) + has_down.astype(jnp.int32))
    send_halo(2, 0)
    info.start()
    for load in loads[1:4]:
        load.wait()
    for r in (1, 2):
        products(2, r)
        send_contributions(r)
    loads[4].wait()
    hidden_frames(0)
    send_halo(0, 1)
    receive_halo(2, 0)
    for r in (3, 0):
        products(2, r)
        send_contributions(r)
    for r in (1, 2):
        products(0, r)
    relay(1)
    receive_halo(0, 1)
    for r in (3, 0):
        products(0, r)

    def later_frames(r):
        for t in (2, 3):
            store_second(t, r, zb[t, r, :, 0:128] + zb[t - 1, r, :, 128:256] + zb[t - 2, r, :, 256:384])

    later_frames(3)
    send_second(2, 0)
    relay(2)
    for r in range(3):
        later_frames(r)
    info.wait_recv()
    wanted = jnp.bitwise_and(x - info_r[0, 0] + 32, 3)
    send_up(1, wanted)
    loads[5].wait()
    receive_second(2, 0)
    made = downsample(3, 0)
    eb[0] = made[:half_w].astype(BF16)
    eb[1] = made[half_w:].astype(BF16)
    for copy in direct[ROWS]:
        copy.start()
    enc[...] = downsample(3, 2) + downsample(2, 1)
    relay(3)
    send_up(2, wanted)
    relay(0)
    send_up(3, wanted)

    def earlier_frames(r):
        got = received(r)
        store_second(0, r, zb[0, r, :, 0:128] + got[0])
        store_second(1, r, zb[1, r, :, 0:128] + zb[0, r, :, 128:256] + got[1])

    relay(ROWS)
    earlier_frames(1)
    send_up(0, wanted)
    earlier_frames(2)
    earlier_frames(3)
    send_second(0, 1)
    send_up(ROWS, wanted)
    earlier_frames(0)
    receive_second(0, 1)
    bias2 = b2_ref[...]
    second_out = enc[...] + downsample(1, 0) + bias2
    full = fc_ref[0] >= 4
    first_out = downsample(0, 1) + downsample(1, 2) + bias2
    for i in range(2):
        part = second_out[i * half_w : (i + 1) * half_w]
        out_ref[1, i] = jnp.where(full, part, 0.0).astype(BF16)
    got = received(ROWS)
    for i in range(2):
        out_ref[0, i] = (first_out[i * half_w : (i + 1) * half_w] + got[i]).astype(BF16)

    info.wait_send()
    for c in range(ROWS + 1):
        for copy in direct[c] + relays[c]:
            copy.wait_send()
        ups[c].wait_send()
    for base, batch in ((2, 0), (0, 1)):
        to_up, to_down = halo_copies(base, batch)

        @pl.when(has_up)
        def _():
            to_up.wait_send()

        @pl.when(has_down)
        def _():
            to_down.wait_send()
            second_copy(base, batch).wait_send()


def per_device(n_group, n_row, video, pred_owner, frame_counts, g1, w1, b1, g2, w2, b2):
    frames, rows, width, channels = video.shape
    outputs = w2.shape[-1]
    half_w = width // 2
    vmem = pl.BlockSpec(memory_space=pltpu.VMEM)
    smem = pl.BlockSpec(memory_space=pltpu.SMEM)
    hbm = pl.BlockSpec(memory_space=pl.ANY)
    dma = pltpu.SemaphoreType.DMA
    chunk = pltpu.VMEM((ROWS, 2, width, channels), BF16)
    last = pltpu.VMEM((2, half_w, outputs), BF16)
    return pl.pallas_call(
        functools.partial(kernel, n_group, n_row),
        out_shape=jax.ShapeDtypeStruct((frames // 2, rows // 2, half_w, outputs), BF16),
        in_specs=[hbm, smem, smem, vmem, hbm, vmem, vmem, hbm, vmem],
        out_specs=vmem,
        scratch_shapes=[
            pltpu.VMEM((frames, rows, width, channels), BF16),
            pltpu.VMEM((9 * channels, 3 * channels), BF16),
            pltpu.VMEM((3, 9 * channels, outputs), BF16),
            pltpu.VMEM((frames, rows + 2, width, 3 * channels), BF16),
            pltpu.VMEM((2, frames, width, channels), BF16),
            pltpu.VMEM((frames, rows, width, 3 * channels), F32),
            pltpu.VMEM((2, width, channels), F32),
            pltpu.VMEM((frames, rows + 1, half_w, 3 * channels), BF16),
            pltpu.VMEM((frames, half_w, 2 * channels), BF16),
            pltpu.VMEM((2 * half_w, outputs), F32),
            chunk, chunk, chunk, chunk, chunk, chunk,
            last, last, last, last, last, last,
            pltpu.VMEM((8, 128), jnp.int32),
            pltpu.VMEM((8, 128), jnp.int32),
            dma((6,)),
            dma((2, 2)), dma((2, 2)),
            dma((2,)), dma((2,)),
            dma((1,)), dma((1,)),
            dma((5, 2)), dma((5, 2)),
            dma((5, 2)), dma((5, 2)),
            dma((5,)), dma((5,)),
        ],
        compiler_params=pltpu.CompilerParams(collective_id=0, has_side_effects=True),
    )(
        video, pred_owner, frame_counts, g1.reshape(1, channels), w1.reshape(3, 9 * channels, channels),
        b1.reshape(1, channels), g2.reshape(1, channels), w2.reshape(3, 9 * channels, outputs),
        b2.reshape(1, outputs),
    )


def solution(mesh):
    placed = (P("group", "row", None, None), P("group"), P("group"), P(), P(), P(), P(), P(), P())
    return jax.shard_map(
        functools.partial(per_device, mesh.shape["group"], mesh.shape["row"]),
        mesh=mesh,
        in_specs=placed,
        out_specs=P("group", "row", None, None),
        check_vma=False,
    )
```

```python
import functools

import jax
import jax.numpy as jnp
from jax import lax
from jax.experimental import pallas as pl
from jax.experimental.pallas import tpu as pltpu
from jax.sharding import PartitionSpec as P

MESH = pl.DeviceIdType.MESH
NX = 4
ROWS = 4
F32 = jnp.float32
BF16 = jnp.bfloat16


def prepare(v, gain):
    inverse = lax.rsqrt(jnp.mean(v * v, axis=-1, keepdims=True) + 1e-06)
    half = v * inverse * (0.5 * gain)
    return half * (1.0 + jnp.tanh(half))


def kernel(
    n_group, n_row, x_hbm, po_ref, fc_ref, g1_ref, w1_hbm, b1_ref, g2_ref, w2_hbm, b2_ref, out_ref,
    xv, w1v, w2v, hid, hin, zb, tmp, sec, sin, enc,
    tb, rl, rr, r2, zs, zr, eb, el, er, e2, es, ez, info_s, info_r,
    lsem, hsend, hrecv, ssend, srecv, isend, irecv, xsend, xrecv, ysend, yrecv, zsend, zrecv,
):
    width = xv.shape[2]
    half_w = width // 2
    n_z = n_group // NX
    me = lax.axis_index("group")
    row = lax.axis_index("row")
    z = me // NX
    x = me % NX
    right = (z * NX + (x + 1) % NX, row)
    left = (z * NX + (x + 3) % NX, row)
    above_z = (jnp.minimum(z + 1, n_z - 1) * NX + x, row)
    below_z = (jnp.maximum(z - 1, 0) * NX + x, row)
    up = (me, jnp.maximum(row - 1, 0))
    down = (me, jnp.minimum(row + 1, n_row - 1))
    has_up = row > 0
    has_down = row < n_row - 1
    has_above = z < n_z - 1
    has_below = z > 0

    barrier = pltpu.get_barrier_semaphore()
    for dev in (right, left):
        pl.semaphore_signal(barrier, inc=1, device_id=dev, device_id_type=MESH)

    @pl.when(has_above)
    def _():
        pl.semaphore_signal(barrier, inc=1, device_id=above_z, device_id_type=MESH)

    @pl.when(has_below)
    def _():
        pl.semaphore_signal(barrier, inc=1, device_id=below_z, device_id_type=MESH)

    @pl.when(has_up)
    def _():
        pl.semaphore_signal(barrier, inc=1, device_id=up, device_id_type=MESH)

    @pl.when(has_down)
    def _():
        pl.semaphore_signal(barrier, inc=1, device_id=down, device_id_type=MESH)

    loads = [
        pltpu.make_async_copy(x_hbm.at[2:4], xv.at[2:4], lsem.at[0]),
        pltpu.make_async_copy(w1_hbm.at[2], w1v.at[:, 0:128], lsem.at[1]),
        pltpu.make_async_copy(w1_hbm.at[1], w1v.at[:, 128:256], lsem.at[2]),
        pltpu.make_async_copy(w1_hbm.at[0], w1v.at[:, 256:384], lsem.at[3]),
        pltpu.make_async_copy(x_hbm.at[0:2], xv.at[0:2], lsem.at[4]),
        pltpu.make_async_copy(w2_hbm, w2v, lsem.at[5]),
    ]
    for load in loads:
        load.start()

    pred = po_ref[0]
    info_s[...] = jnp.full((8, 128), pred, jnp.int32)

    columns = lax.broadcasted_iota(jnp.int32, (width, 128), 0)
    half_columns = lax.broadcasted_iota(jnp.int32, (half_w, 128), 0)

    def store_hidden(f, r, h):
        before = jnp.where(columns == 0, 0.0, pltpu.roll(h, 1, 0))
        after = jnp.where(columns == width - 1, 0.0, pltpu.roll(h, width - 1, 0))
        hid[f, r, :, 0:128] = before.astype(BF16)
        hid[f, r, :, 128:256] = h.astype(BF16)
        hid[f, r, :, 256:384] = after.astype(BF16)

    gain1 = g1_ref[...]
    gain2 = g2_ref[...]

    def hidden_frames(base):
        def step(i, carry):
            f = base + i // ROWS
            r = i % ROWS
            store_hidden(f, r + 1, prepare(xv[f, r].astype(F32), gain1))
            return carry

        lax.fori_loop(0, 2 * ROWS, step, 0, unroll=2)

    def halo_copies(base, batch):
        to_up = pltpu.make_async_remote_copy(
            src_ref=hid.at[base : base + 2, 1, :, 128:256], dst_ref=hin.at[1, base : base + 2],
            send_sem=hsend.at[batch, 0], recv_sem=hrecv.at[batch, 1], device_id=up, device_id_type=MESH,
        )
        to_down = pltpu.make_async_remote_copy(
            src_ref=hid.at[base : base + 2, ROWS, :, 128:256], dst_ref=hin.at[0, base : base + 2],
            send_sem=hsend.at[batch, 1], recv_sem=hrecv.at[batch, 0], device_id=down, device_id_type=MESH,
        )
        return to_up, to_down

    def send_halo(base, batch):
        to_up, to_down = halo_copies(base, batch)

        @pl.when(has_up)
        def _():
            to_up.start()

        @pl.when(has_down)
        def _():
            to_down.start()

    def receive_halo(base, batch):
        to_up, to_down = halo_copies(base, batch)

        @pl.when(has_up)
        def _():
            to_down.wait_recv()
            for f in (base, base + 1):
                store_hidden(f, 0, hin[0, f].astype(F32))

        @pl.when(has_down)
        def _():
            to_up.wait_recv()
            for f in (base, base + 1):
                store_hidden(f, ROWS + 1, hin[1, f].astype(F32))

        @pl.when(row == 0)
        def _():
            for f in (base, base + 1):
                hid[f, 0] = jnp.zeros((width, 384), BF16)

        @pl.when(row == n_row - 1)
        def _():
            for f in (base, base + 1):
                hid[f, ROWS + 1] = jnp.zeros((width, 384), BF16)

    def products(base, r):
        lhs = jnp.concatenate(
            [
                jnp.concatenate([hid[f, r + b] for b in range(3)], axis=1)
                for f in (base, base + 1)
            ],
            axis=0,
        )
        made = jnp.dot(lhs, w1v[...], preferred_element_type=F32)
        zb[base, r] = made[:width]
        zb[base + 1, r] = made[width:]

    def direct_copies(src, from_left, from_right, c):
        return (
            pltpu.make_async_remote_copy(
                src_ref=src, dst_ref=from_left, send_sem=xsend.at[c, 0], recv_sem=xrecv.at[c, 0],
                device_id=right, device_id_type=MESH,
            ),
            pltpu.make_async_remote_copy(
                src_ref=src, dst_ref=from_right, send_sem=xsend.at[c, 1], recv_sem=xrecv.at[c, 1],
                device_id=left, device_id_type=MESH,
            ),
        )

    def relay_copies(from_left, from_right, far, c):
        return (
            pltpu.make_async_remote_copy(
                src_ref=from_left.at[0], dst_ref=far.at[0], send_sem=ysend.at[c, 0], recv_sem=yrecv.at[c, 0],
                device_id=right, device_id_type=MESH,
            ),
            pltpu.make_async_remote_copy(
                src_ref=from_right.at[1], dst_ref=far.at[1], send_sem=ysend.at[c, 1], recv_sem=yrecv.at[c, 1],
                device_id=left, device_id_type=MESH,
            ),
        )

    def z_copy(src, dst, c):
        return pltpu.make_async_remote_copy(
            src_ref=src, dst_ref=dst, send_sem=zsend.at[c], recv_sem=zrecv.at[c],
            device_id=above_z, device_id_type=MESH,
        )

    info = pltpu.make_async_remote_copy(
        src_ref=info_s, dst_ref=info_r, send_sem=isend.at[0], recv_sem=irecv.at[0],
        device_id=below_z, device_id_type=MESH,
    )
    direct = [direct_copies(tb.at[c], rl.at[c], rr.at[c], c) for c in range(ROWS)]
    direct.append(direct_copies(eb, el, er, ROWS))
    relays = [relay_copies(rl.at[c], rr.at[c], r2.at[c], c) for c in range(ROWS)]
    relays.append(relay_copies(el, er, e2, ROWS))
    ups = [z_copy(zs.at[c], zr.at[c], c) for c in range(ROWS)]
    ups.append(z_copy(es, ez, ROWS))

    def send_contributions(r):
        tb[r, 0] = (zb[2, r, :, 256:384] + zb[3, r, :, 128:256]).astype(BF16)
        tb[r, 1] = zb[3, r, :, 256:384].astype(BF16)
        for copy in direct[r]:
            copy.start()

    def relay(c):
        for copy, on in zip(direct[c], relays[c]):
            copy.wait_recv()
            on.start()

    def pick(c, which, own, from_left, far, from_right):
        kept = jnp.where(which == 0, own[...], from_left[...])
        kept = jnp.where(which == 2, far[...], kept)
        return jnp.where(which == 3, from_right[...], kept)

    def send_up(c):
        for copy in relays[c]:
            copy.wait_recv()

        @pl.when(has_above)
        def _():
            which = jnp.bitwise_and(x - info_r[0, 0] + 32, 3)
            if c < ROWS:
                zs[c] = pick(c, which, tb.at[c], rl.at[c], r2.at[c], rr.at[c])
            else:
                es[...] = pick(c, which, eb, el, e2, er)
            ups[c].start()

    distance = me - pred
    choice = jnp.where(pred < 0, 5, jnp.where(distance <= x, distance, 0))

    def received(c):
        @pl.when(has_below)
        def _():
            ups[c].wait_recv()

        if c < ROWS:
            got = pick(c, choice, zr.at[c], rl.at[c], r2.at[c], rr.at[c])
        else:
            got = pick(c, choice, ez, el, e2, er)
        got = got.astype(F32)
        return jnp.where(choice == 5, 0.0, got)

    bias1 = b1_ref[...]

    def store_second(t, r, mixed):
        v = xv[t, r].astype(F32) + mixed + bias1
        slot = tmp.at[t % 2]
        slot[...] = prepare(v, gain2)
        even = slot[pl.ds(0, half_w, stride=2), :]
        odd = slot[pl.ds(1, half_w, stride=2), :]
        sec[t, r + 1, :, 0:128] = jnp.where(half_columns == 0, 0.0, pltpu.roll(odd, 1, 0)).astype(BF16)
        sec[t, r + 1, :, 128:256] = even.astype(BF16)
        sec[t, r + 1, :, 256:384] = odd.astype(BF16)

    def second_copy(base, batch):
        return pltpu.make_async_remote_copy(
            src_ref=sec.at[base : base + 2, ROWS, :, 128:384], dst_ref=sin.at[base : base + 2],
            send_sem=ssend.at[batch], recv_sem=srecv.at[batch], device_id=down, device_id_type=MESH,
        )

    def send_second(base, batch):
        @pl.when(has_down)
        def _():
            second_copy(base, batch).start()

    def receive_second(base, batch):
        @pl.when(has_up)
        def _():
            second_copy(base, batch).wait_recv()
            for t in (base, base + 1):
                odd = sin[t, :, 128:256].astype(F32)
                sec[t, 0, :, 0:128] = jnp.where(half_columns == 0, 0.0, pltpu.roll(odd, 1, 0)).astype(BF16)
                sec[t, 0, :, 128:384] = sin[t]

        @pl.when(row == 0)
        def _():
            for t in (base, base + 1):
                sec[t, 0] = jnp.zeros((half_w, 384), BF16)

    def downsample(t, a):
        lhs = jnp.concatenate(
            [
                jnp.concatenate([sec[t, 2 * i + b] for b in range(3)], axis=1)
                for i in range(2)
            ],
            axis=0,
        )
        return jnp.dot(lhs, w2v[a], preferred_element_type=F32)

    loads[0].wait()
    hidden_frames(2)
    expected = sum(flag.astype(jnp.int32) for flag in (has_up, has_down, has_above, has_below))
    pl.semaphore_wait(barrier, 2 + expected)
    send_halo(2, 0)

    @pl.when(has_below)
    def _():
        info.start()

    @pl.when(jnp.logical_not(has_below))
    def _():
        zr[...] = jnp.zeros_like(zr)
        ez[...] = jnp.zeros_like(ez)

    for load in loads[1:4]:
        load.wait()
    for r in (1, 2):
        products(2, r)
        send_contributions(r)
    loads[4].wait()
    hidden_frames(0)
    send_halo(0, 1)
    receive_halo(2, 0)
    for r in (3, 0):
        products(2, r)
        send_contributions(r)
    for r in (1, 2):
        products(0, r)
    relay(1)
    receive_halo(0, 1)
    for r in (3, 0):
        products(0, r)

    def later_frames(r):
        for t in (2, 3):
            store_second(t, r, zb[t, r, :, 0:128] + zb[t - 1, r, :, 128:256] + zb[t - 2, r, :, 256:384])

    later_frames(3)
    send_second(2, 0)
    relay(2)
    for r in range(3):
        later_frames(r)

    @pl.when(has_above)
    def _():
        info.wait_recv()

    send_up(1)
    loads[5].wait()
    receive_second(2, 0)
    made = downsample(3, 0)
    eb[0] = made[:half_w].astype(BF16)
    eb[1] = made[half_w:].astype(BF16)
    for copy in direct[ROWS]:
        copy.start()
    enc[...] = downsample(3, 2) + downsample(2, 1)
    relay(3)
    send_up(2)
    relay(0)
    send_up(3)

    def earlier_frames(r):
        got = received(r)
        store_second(0, r, zb[0, r, :, 0:128] + got[0])
        store_second(1, r, zb[1, r, :, 0:128] + zb[0, r, :, 128:256] + got[1])

    relay(ROWS)
    earlier_frames(1)
    send_up(0)
    earlier_frames(2)
    earlier_frames(3)
    send_second(0, 1)
    send_up(ROWS)
    earlier_frames(0)
    receive_second(0, 1)
    bias2 = b2_ref[...]
    second_out = enc[...] + downsample(1, 0) + bias2
    full = fc_ref[0] >= 4
    first_out = downsample(0, 1) + downsample(1, 2) + bias2
    for i in range(2):
        part = second_out[i * half_w : (i + 1) * half_w]
        out_ref[1, i] = jnp.where(full, part, 0.0).astype(BF16)
    got = received(ROWS)
    for i in range(2):
        out_ref[0, i] = (first_out[i * half_w : (i + 1) * half_w] + got[i]).astype(BF16)

    @pl.when(has_below)
    def _():
        info.wait_send()

    @pl.when(has_above)
    def _():
        for c in range(ROWS + 1):
            ups[c].wait_send()

    for c in range(ROWS + 1):
        for copy in direct[c] + relays[c]:
            copy.wait_send()
    for base, batch in ((2, 0), (0, 1)):
        to_up, to_down = halo_copies(base, batch)

        @pl.when(has_up)
        def _():
            to_up.wait_send()

        @pl.when(has_down)
        def _():
            to_down.wait_send()
            second_copy(base, batch).wait_send()


def per_device(n_group, n_row, video, pred_owner, frame_counts, g1, w1, b1, g2, w2, b2):
    frames, rows, width, channels = video.shape
    outputs = w2.shape[-1]
    half_w = width // 2
    vmem = pl.BlockSpec(memory_space=pltpu.VMEM)
    smem = pl.BlockSpec(memory_space=pltpu.SMEM)
    hbm = pl.BlockSpec(memory_space=pl.ANY)
    dma = pltpu.SemaphoreType.DMA
    chunk = pltpu.VMEM((ROWS, 2, width, channels), BF16)
    last = pltpu.VMEM((2, half_w, outputs), BF16)
    return pl.pallas_call(
        functools.partial(kernel, n_group, n_row),
        out_shape=jax.ShapeDtypeStruct((frames // 2, rows // 2, half_w, outputs), BF16),
        in_specs=[hbm, smem, smem, vmem, hbm, vmem, vmem, hbm, vmem],
        out_specs=vmem,
        scratch_shapes=[
            pltpu.VMEM((frames, rows, width, channels), BF16),
            pltpu.VMEM((9 * channels, 3 * channels), BF16),
            pltpu.VMEM((3, 9 * channels, outputs), BF16),
            pltpu.VMEM((frames, rows + 2, width, 3 * channels), BF16),
            pltpu.VMEM((2, frames, width, channels), BF16),
            pltpu.VMEM((frames, rows, width, 3 * channels), F32),
            pltpu.VMEM((2, width, channels), F32),
            pltpu.VMEM((frames, rows + 1, half_w, 3 * channels), BF16),
            pltpu.VMEM((frames, half_w, 2 * channels), BF16),
            pltpu.VMEM((2 * half_w, outputs), F32),
            chunk, chunk, chunk, chunk, chunk, chunk,
            last, last, last, last, last, last,
            pltpu.VMEM((8, 128), jnp.int32),
            pltpu.VMEM((8, 128), jnp.int32),
            dma((6,)),
            dma((2, 2)), dma((2, 2)),
            dma((2,)), dma((2,)),
            dma((1,)), dma((1,)),
            dma((5, 2)), dma((5, 2)),
            dma((5, 2)), dma((5, 2)),
            dma((5,)), dma((5,)),
        ],
        compiler_params=pltpu.CompilerParams(collective_id=0, has_side_effects=True),
    )(
        video, pred_owner, frame_counts, g1.reshape(1, channels), w1.reshape(3, 9 * channels, channels),
        b1.reshape(1, channels), g2.reshape(1, channels), w2.reshape(3, 9 * channels, outputs),
        b2.reshape(1, outputs),
    )


def solution(mesh):
    placed = (P("group", "row", None, None), P("group"), P("group"), P(), P(), P(), P(), P(), P())
    return jax.shard_map(
        functools.partial(per_device, mesh.shape["group"], mesh.shape["row"]),
        mesh=mesh,
        in_specs=placed,
        out_specs=P("group", "row", None, None),
        check_vma=False,
    )
```

```python
import functools

import jax
import jax.numpy as jnp
from jax import lax
from jax.experimental import pallas as pl
from jax.experimental.pallas import tpu as pltpu
from jax.sharding import PartitionSpec as P

MESH = pl.DeviceIdType.MESH
NX = 4
ROWS = 4
F32 = jnp.float32
BF16 = jnp.bfloat16


def prepare(v, gain):
    inverse = lax.rsqrt(jnp.mean(v * v, axis=-1, keepdims=True) + 1e-06)
    half = v * inverse * (0.5 * gain)
    return half * (1.0 + jnp.tanh(half))


def kernel(
    n_group, n_row, x_hbm, po_ref, fc_ref, g1_ref, w1_hbm, b1_ref, g2_ref, w2_hbm, b2_ref, out_ref,
    xv, w1v, w2v, hid, hin, zb, tmp, sec, sin, enc,
    tb, rl, rr, r2, zs, zr, eb, el, er, e2, es, ez, info_s, info_r,
    lsem, hsend, hrecv, ssend, srecv, isend, irecv, xsend, xrecv, ysend, yrecv, zsend, zrecv,
):
    width = xv.shape[2]
    half_w = width // 2
    n_z = n_group // NX
    me = lax.axis_index("group")
    row = lax.axis_index("row")
    z = me // NX
    x = me % NX
    right = (z * NX + (x + 1) % NX, row)
    left = (z * NX + (x + 3) % NX, row)
    above_z = (jnp.minimum(z + 1, n_z - 1) * NX + x, row)
    below_z = (jnp.maximum(z - 1, 0) * NX + x, row)
    up = (me, jnp.maximum(row - 1, 0))
    down = (me, jnp.minimum(row + 1, n_row - 1))
    has_up = row > 0
    has_down = row < n_row - 1
    has_above = z < n_z - 1
    has_below = z > 0

    barrier = pltpu.get_barrier_semaphore()
    for dev in (right, left):
        pl.semaphore_signal(barrier, inc=1, device_id=dev, device_id_type=MESH)

    @pl.when(has_above)
    def _():
        pl.semaphore_signal(barrier, inc=1, device_id=above_z, device_id_type=MESH)

    @pl.when(has_below)
    def _():
        pl.semaphore_signal(barrier, inc=1, device_id=below_z, device_id_type=MESH)

    @pl.when(has_up)
    def _():
        pl.semaphore_signal(barrier, inc=1, device_id=up, device_id_type=MESH)

    @pl.when(has_down)
    def _():
        pl.semaphore_signal(barrier, inc=1, device_id=down, device_id_type=MESH)

    loads = [
        pltpu.make_async_copy(x_hbm.at[2:4], xv.at[2:4], lsem.at[0]),
        pltpu.make_async_copy(w1_hbm.at[2], w1v.at[:, 0:128], lsem.at[1]),
        pltpu.make_async_copy(w1_hbm.at[1], w1v.at[:, 128:256], lsem.at[2]),
        pltpu.make_async_copy(w1_hbm.at[0], w1v.at[:, 256:384], lsem.at[3]),
        pltpu.make_async_copy(x_hbm.at[0:2], xv.at[0:2], lsem.at[4]),
        pltpu.make_async_copy(w2_hbm, w2v, lsem.at[5]),
    ]
    for load in loads:
        load.start()

    pred = po_ref[0]
    info_s[...] = jnp.full((8, 128), pred, jnp.int32)

    columns = lax.broadcasted_iota(jnp.int32, (width, 128), 0)
    half_columns = lax.broadcasted_iota(jnp.int32, (half_w, 128), 0)

    def store_hidden(f, r, h):
        before = jnp.where(columns == 0, 0.0, pltpu.roll(h, 1, 0))
        after = jnp.where(columns == width - 1, 0.0, pltpu.roll(h, width - 1, 0))
        hid[f, r, :, 0:128] = before.astype(BF16)
        hid[f, r, :, 128:256] = h.astype(BF16)
        hid[f, r, :, 256:384] = after.astype(BF16)

    gain1 = g1_ref[...]
    gain2 = g2_ref[...]

    def hidden_frames(base):
        def step(i, carry):
            f = base + i // ROWS
            r = i % ROWS
            store_hidden(f, r + 1, prepare(xv[f, r].astype(F32), gain1))
            return carry

        lax.fori_loop(0, 2 * ROWS, step, 0, unroll=2)

    def halo_copies(base, batch):
        to_up = pltpu.make_async_remote_copy(
            src_ref=hid.at[base : base + 2, 1, :, 128:256], dst_ref=hin.at[1, base : base + 2],
            send_sem=hsend.at[batch, 0], recv_sem=hrecv.at[batch, 1], device_id=up, device_id_type=MESH,
        )
        to_down = pltpu.make_async_remote_copy(
            src_ref=hid.at[base : base + 2, ROWS, :, 128:256], dst_ref=hin.at[0, base : base + 2],
            send_sem=hsend.at[batch, 1], recv_sem=hrecv.at[batch, 0], device_id=down, device_id_type=MESH,
        )
        return to_up, to_down

    def send_halo(base, batch):
        to_up, to_down = halo_copies(base, batch)

        @pl.when(has_up)
        def _():
            to_up.start()

        @pl.when(has_down)
        def _():
            to_down.start()

    def receive_halo(base, batch):
        to_up, to_down = halo_copies(base, batch)

        @pl.when(has_up)
        def _():
            to_down.wait_recv()
            for f in (base, base + 1):
                store_hidden(f, 0, hin[0, f].astype(F32))

        @pl.when(has_down)
        def _():
            to_up.wait_recv()
            for f in (base, base + 1):
                store_hidden(f, ROWS + 1, hin[1, f].astype(F32))

        @pl.when(row == 0)
        def _():
            for f in (base, base + 1):
                hid[f, 0] = jnp.zeros((width, 384), BF16)

        @pl.when(row == n_row - 1)
        def _():
            for f in (base, base + 1):
                hid[f, ROWS + 1] = jnp.zeros((width, 384), BF16)

    def products(base, r):
        lhs = jnp.concatenate(
            [
                jnp.concatenate([hid[f, r + b] for b in range(3)], axis=1)
                for f in (base, base + 1)
            ],
            axis=0,
        )
        made = jnp.dot(lhs, w1v[...], preferred_element_type=F32)
        zb[base, r] = made[:width]
        zb[base + 1, r] = made[width:]

    def direct_copies(src, from_left, from_right, c):
        return [
            [
                pltpu.make_async_remote_copy(
                    src_ref=src.at[half], dst_ref=into.at[half],
                    send_sem=xsend.at[c, side, half], recv_sem=xrecv.at[c, side, half],
                    device_id=dev, device_id_type=MESH,
                )
                for half in order
            ]
            for side, into, dev, order in ((0, from_left, right, (0, 1)), (1, from_right, left, (1, 0)))
        ]

    def relay_copies(from_left, from_right, far, c):
        return (
            pltpu.make_async_remote_copy(
                src_ref=from_left.at[0], dst_ref=far.at[0], send_sem=ysend.at[c, 0], recv_sem=yrecv.at[c, 0],
                device_id=right, device_id_type=MESH,
            ),
            pltpu.make_async_remote_copy(
                src_ref=from_right.at[1], dst_ref=far.at[1], send_sem=ysend.at[c, 1], recv_sem=yrecv.at[c, 1],
                device_id=left, device_id_type=MESH,
            ),
        )

    def z_copy(src, dst, c):
        return pltpu.make_async_remote_copy(
            src_ref=src, dst_ref=dst, send_sem=zsend.at[c], recv_sem=zrecv.at[c],
            device_id=above_z, device_id_type=MESH,
        )

    info = pltpu.make_async_remote_copy(
        src_ref=info_s, dst_ref=info_r, send_sem=isend.at[0], recv_sem=irecv.at[0],
        device_id=below_z, device_id_type=MESH,
    )
    direct = [direct_copies(tb.at[c], rl.at[c], rr.at[c], c) for c in range(ROWS)]
    direct.append(direct_copies(eb, el, er, ROWS))
    relays = [relay_copies(rl.at[c], rr.at[c], r2.at[c], c) for c in range(ROWS)]
    relays.append(relay_copies(el, er, e2, ROWS))
    ups = [z_copy(zs.at[c], zr.at[c], c) for c in range(ROWS)]
    ups.append(z_copy(es, ez, ROWS))

    def contributions(r):
        tb[r, 0] = (zb[2, r, :, 256:384] + zb[3, r, :, 128:256]).astype(BF16)
        tb[r, 1] = zb[3, r, :, 256:384].astype(BF16)

    def send_direct(c, turns=(0, 1)):
        for turn in turns:
            for copies in direct[c]:
                copies[turn].start()

    def relay(c):
        for copies, on in zip(direct[c], relays[c]):
            copies[0].wait_recv()
            on.start()

    def pick(c, which, own, from_left, far, from_right):
        kept = jnp.where(which == 0, own[...], from_left[...])
        kept = jnp.where(which == 2, far[...], kept)
        return jnp.where(which == 3, from_right[...], kept)

    def send_up(c):
        for copies, copy in zip(direct[c], relays[c]):
            copies[1].wait_recv()
            copy.wait_recv()

        @pl.when(has_above)
        def _():
            which = jnp.bitwise_and(x - info_r[0, 0] + 32, 3)
            if c < ROWS:
                zs[c] = pick(c, which, tb.at[c], rl.at[c], r2.at[c], rr.at[c])
            else:
                es[...] = pick(c, which, eb, el, e2, er)
            ups[c].start()

    distance = me - pred
    choice = jnp.where(pred < 0, 5, jnp.where(distance <= x, distance, 0))

    def received(c):
        @pl.when(has_below)
        def _():
            ups[c].wait_recv()

        if c < ROWS:
            got = pick(c, choice, zr.at[c], rl.at[c], r2.at[c], rr.at[c])
        else:
            got = pick(c, choice, ez, el, e2, er)
        got = got.astype(F32)
        return jnp.where(choice == 5, 0.0, got)

    bias1 = b1_ref[...]

    def store_second(t, r, mixed):
        v = xv[t, r].astype(F32) + mixed + bias1
        slot = tmp.at[t % 2]
        slot[...] = prepare(v, gain2)
        even = slot[pl.ds(0, half_w, stride=2), :]
        odd = slot[pl.ds(1, half_w, stride=2), :]
        sec[t, r + 1, :, 0:128] = jnp.where(half_columns == 0, 0.0, pltpu.roll(odd, 1, 0)).astype(BF16)
        sec[t, r + 1, :, 128:256] = even.astype(BF16)
        sec[t, r + 1, :, 256:384] = odd.astype(BF16)

    def second_copy(base, batch):
        return pltpu.make_async_remote_copy(
            src_ref=sec.at[base : base + 2, ROWS, :, 128:384], dst_ref=sin.at[base : base + 2],
            send_sem=ssend.at[batch], recv_sem=srecv.at[batch], device_id=down, device_id_type=MESH,
        )

    def send_second(base, batch):
        @pl.when(has_down)
        def _():
            second_copy(base, batch).start()

    def receive_second(base, batch):
        @pl.when(has_up)
        def _():
            second_copy(base, batch).wait_recv()
            for t in (base, base + 1):
                odd = sin[t, :, 128:256].astype(F32)
                sec[t, 0, :, 0:128] = jnp.where(half_columns == 0, 0.0, pltpu.roll(odd, 1, 0)).astype(BF16)
                sec[t, 0, :, 128:384] = sin[t]

        @pl.when(row == 0)
        def _():
            for t in (base, base + 1):
                sec[t, 0] = jnp.zeros((half_w, 384), BF16)

    def downsample(t, a):
        lhs = jnp.concatenate(
            [
                jnp.concatenate([sec[t, 2 * i + b] for b in range(3)], axis=1)
                for i in range(2)
            ],
            axis=0,
        )
        return jnp.dot(lhs, w2v[a], preferred_element_type=F32)

    loads[0].wait()
    hidden_frames(2)
    expected = sum(flag.astype(jnp.int32) for flag in (has_up, has_down, has_above, has_below))
    pl.semaphore_wait(barrier, 2 + expected)
    send_halo(2, 0)

    @pl.when(has_below)
    def _():
        info.start()

    @pl.when(jnp.logical_not(has_below))
    def _():
        zr[...] = jnp.zeros_like(zr)
        ez[...] = jnp.zeros_like(ez)

    for load in loads[1:4]:
        load.wait()

    def later_frames(r):
        for t in (2, 3):
            store_second(t, r, zb[t, r, :, 0:128] + zb[t - 1, r, :, 128:256] + zb[t - 2, r, :, 256:384])

    def earlier_frames(r):
        got = received(r)
        store_second(0, r, zb[0, r, :, 0:128] + got[0])
        store_second(1, r, zb[1, r, :, 0:128] + zb[0, r, :, 128:256] + got[1])

    for r in (1, 2):
        products(2, r)
        contributions(r)
        send_direct(r)
    loads[4].wait()
    hidden_frames(0)
    send_halo(0, 1)
    receive_halo(2, 0)
    products(2, 3)
    contributions(3)
    relay(1)
    send_direct(3)
    products(2, 0)
    contributions(0)
    for r in (1, 2):
        products(0, r)
    receive_halo(0, 1)
    relay(2)
    send_direct(0)
    for r in (3, 0):
        products(0, r)
    later_frames(3)
    send_second(2, 0)
    for r in range(3):
        later_frames(r)

    @pl.when(has_above)
    def _():
        info.wait_recv()

    send_up(1)
    relay(3)
    loads[5].wait()
    receive_second(2, 0)
    made = downsample(3, 0)
    eb[0] = made[:half_w].astype(BF16)
    eb[1] = made[half_w:].astype(BF16)
    send_direct(ROWS, (0,))
    enc[...] = downsample(3, 2) + downsample(2, 1)
    send_up(2)
    relay(0)
    send_direct(ROWS, (1,))
    earlier_frames(1)
    send_up(3)
    earlier_frames(2)
    relay(ROWS)
    send_up(0)
    earlier_frames(3)
    send_second(0, 1)
    send_up(ROWS)
    earlier_frames(0)
    receive_second(0, 1)
    bias2 = b2_ref[...]
    second_out = enc[...] + downsample(1, 0) + bias2
    full = fc_ref[0] >= 4
    first_out = downsample(0, 1) + downsample(1, 2) + bias2
    for i in range(2):
        part = second_out[i * half_w : (i + 1) * half_w]
        out_ref[1, i] = jnp.where(full, part, 0.0).astype(BF16)
    got = received(ROWS)
    for i in range(2):
        out_ref[0, i] = (first_out[i * half_w : (i + 1) * half_w] + got[i]).astype(BF16)

    @pl.when(has_below)
    def _():
        info.wait_send()

    @pl.when(has_above)
    def _():
        for c in range(ROWS + 1):
            ups[c].wait_send()

    for c in range(ROWS + 1):
        for copy in direct[c][0] + direct[c][1] + list(relays[c]):
            copy.wait_send()
    for base, batch in ((2, 0), (0, 1)):
        to_up, to_down = halo_copies(base, batch)

        @pl.when(has_up)
        def _():
            to_up.wait_send()

        @pl.when(has_down)
        def _():
            to_down.wait_send()
            second_copy(base, batch).wait_send()


def per_device(n_group, n_row, video, pred_owner, frame_counts, g1, w1, b1, g2, w2, b2):
    frames, rows, width, channels = video.shape
    outputs = w2.shape[-1]
    half_w = width // 2
    vmem = pl.BlockSpec(memory_space=pltpu.VMEM)
    smem = pl.BlockSpec(memory_space=pltpu.SMEM)
    hbm = pl.BlockSpec(memory_space=pl.ANY)
    dma = pltpu.SemaphoreType.DMA
    chunk = pltpu.VMEM((ROWS, 2, width, channels), BF16)
    last = pltpu.VMEM((2, half_w, outputs), BF16)
    return pl.pallas_call(
        functools.partial(kernel, n_group, n_row),
        out_shape=jax.ShapeDtypeStruct((frames // 2, rows // 2, half_w, outputs), BF16),
        in_specs=[hbm, smem, smem, vmem, hbm, vmem, vmem, hbm, vmem],
        out_specs=vmem,
        scratch_shapes=[
            pltpu.VMEM((frames, rows, width, channels), BF16),
            pltpu.VMEM((9 * channels, 3 * channels), BF16),
            pltpu.VMEM((3, 9 * channels, outputs), BF16),
            pltpu.VMEM((frames, rows + 2, width, 3 * channels), BF16),
            pltpu.VMEM((2, frames, width, channels), BF16),
            pltpu.VMEM((frames, rows, width, 3 * channels), F32),
            pltpu.VMEM((2, width, channels), F32),
            pltpu.VMEM((frames, rows + 1, half_w, 3 * channels), BF16),
            pltpu.VMEM((frames, half_w, 2 * channels), BF16),
            pltpu.VMEM((2 * half_w, outputs), F32),
            chunk, chunk, chunk, chunk, chunk, chunk,
            last, last, last, last, last, last,
            pltpu.VMEM((8, 128), jnp.int32),
            pltpu.VMEM((8, 128), jnp.int32),
            dma((6,)),
            dma((2, 2)), dma((2, 2)),
            dma((2,)), dma((2,)),
            dma((1,)), dma((1,)),
            dma((5, 2, 2)), dma((5, 2, 2)),
            dma((5, 2)), dma((5, 2)),
            dma((5,)), dma((5,)),
        ],
        compiler_params=pltpu.CompilerParams(collective_id=0, has_side_effects=True),
    )(
        video, pred_owner, frame_counts, g1.reshape(1, channels), w1.reshape(3, 9 * channels, channels),
        b1.reshape(1, channels), g2.reshape(1, channels), w2.reshape(3, 9 * channels, outputs),
        b2.reshape(1, outputs),
    )


def solution(mesh):
    placed = (P("group", "row", None, None), P("group"), P("group"), P(), P(), P(), P(), P(), P())
    return jax.shard_map(
        functools.partial(per_device, mesh.shape["group"], mesh.shape["row"]),
        mesh=mesh,
        in_specs=placed,
        out_specs=P("group", "row", None, None),
        check_vma=False,
    )
```
